32 devices in a mesh: grp: 2 (over y), leaf: 4 (over z), limb: 2 (over x), coef: 2 (over core).
Axes of the slice: x: 2, y: 2, z: 4, core: 2. Of those that a mesh axis runs over, the one named last changes fastest.
Arguments:
- root_keys: bfloat16 [8, 1, 2, 12, 256, 128], P(('grp', 'leaf'), None, None, 'limb', 'coef'), parts along dimension 0, may hold values from -6 to 6
- switch_main: bfloat16 [8, 2, 4, 2, 12, 256, 128], P(('grp', 'leaf'), None, None, None, 'limb', 'coef'), parts along dimension 0, may hold values from -3 to 3
- switch_special: bfloat16 [8, 2, 4, 2, 4, 256, 128], P(('grp', 'leaf'), None, None, None, 'limb', 'coef'), parts along dimension 0, may hold values from -3 to 3
- basis_up: bfloat16 [4, 16, 3], replicated, may hold values from -3.5 to 3.5
- basis_down: bfloat16 [12, 4], P('limb'), may hold values from -3 to 3
- special_inverse: float32 [12], P('limb'), may hold values from 0.5 to 2
- parent_table: int32 [2, 8], P(None, 'grp'), parts along dimension 1, may hold values from 0 to 3, as said below
- owner_table: int32 [8], P('grp'), parts along dimension 0, may hold values from 0 to 3, as said below
Outputs:
- delivered: bfloat16 [8, 3, 1, 2, 12, 256, 128], P(('grp', 'leaf'), None, None, None, 'limb', 'coef'), parts along dimension 0
The draws below stay inside these ranges and needn't reach their ends.
There are 2 independent parts, one for each index of `grp`. The reference program is written for one: setup_inputs(seed, part) draws one part's arguments, and reference() takes and returns one part's arrays. A program takes and returns all parts, laid end to end along the dimension named above; an argument that names none is the same for every part. Nothing has to cross between parts.
Inputs may be any that keep to these rules, and one draw needn't show every extreme that they name: parent_table[l, j] = (j + e) mod 4 with e from -2 to 2; in every row e = 2 for some j and e = -2 for another j. `owner_table`: each value is taken by at most 3 entries, and by exactly 3 entries for some value.
All inputs are finite; a program needn't handle non-finite values.
Results may differ from the reference program's by a relative error of at most 0.025.
Values may be sent and summed in bfloat16 or wider, within the bound.
No kernel may reach another device: no remote copies, remote signals or barrier semaphores. Data moves between devices by JAX's collectives and lax.ppermute only.
A program may use at most 64 MiB of HBM per device.

```python
import math
import jax
import jax.numpy as jnp
from jax import lax

N1 = 128
N2 = 256
LQ = 12
LP = 4
DIGITS = 4
DLIMBS = 3
COMPS = 1
LEVELS = 2
RADIUS = 2
CAP = 3
LEAVES = 4


def draw_parent_table(key, part):
    parent_rows = []
    for tree_level in range(LEVELS):
        level_key = jax.random.fold_in(key, 101 + tree_level)
        offsets = jax.random.randint(jax.random.fold_in(level_key, 1), (LEAVES,), -RADIUS, RADIUS + 1)
        shuffled = jax.random.permutation(jax.random.fold_in(level_key, 2), LEAVES)
        offsets = offsets.at[shuffled[0]].set(RADIUS).at[shuffled[1]].set(-RADIUS)
        parent_rows.append((jnp.arange(LEAVES) + offsets) % LEAVES)
    return jnp.stack(parent_rows).astype(jnp.int32)


def draw_owner_table(key, part):
    slot_count = LEAVES * CAP
    shuffled = jax.random.permutation(jax.random.fold_in(key, 7), slot_count)
    favoured = shuffled[0] // CAP
    ranking = jnp.argsort(shuffled)
    slot_ids = jnp.arange(slot_count)
    priority = jnp.where(slot_ids // CAP == favoured, -1, ranking)
    chosen = jnp.argsort(priority, stable=True)[:LEAVES]
    owners = chosen // CAP
    mixing = jax.random.permutation(jax.random.fold_in(key, 8), LEAVES)
    return owners[mixing].astype(jnp.int32)


def shard_levels(own_key, dims, shards, low, high):
    def one(axis_at, blocks):
        draws = jax.random.uniform(jax.random.fold_in(jax.random.fold_in(own_key, 6), axis_at), (blocks,), jnp.float32, low / len(shards), high / len(shards))
        return jnp.repeat(jnp.exp(draws), dims[axis_at] // blocks).reshape((-1,) + (1,) * (len(dims) - axis_at - 1))

    factor_of = one(*shards[0])
    for cut in shards[1:]:
        factor_of = factor_of * one(*cut)
    return factor_of


def scatter_about(stream_key, extent, width, bound, pieces=(), kind=jnp.bfloat16):
    values = jax.random.normal(stream_key, extent, jnp.float32) * width
    if len(pieces) > 0:
        values = shard_levels(stream_key, extent, pieces, -0.22, 0.18) * values
    return jnp.clip(values, min=-bound, max=bound).astype(kind)


def setup_inputs(seed: int = 0, part: int = 0) -> dict:
    keys = jax.random.split(jax.random.key(seed), 9)
    own_keys = jax.random.split(jax.random.fold_in(keys[8], part), 9)
    root_keys = scatter_about(own_keys[0], (LEAVES, COMPS, 2, LQ, N2, N1), 1.0, 6.0, ((0, 4), (3, 2), (4, 2)))
    switch_main = scatter_about(own_keys[1], (LEAVES, LEVELS, DIGITS, 2, LQ, N2, N1), DIGITS ** -0.5, 3.0, ((0, 4), (4, 2), (5, 2)))
    switch_special = scatter_about(own_keys[2], (LEAVES, LEVELS, DIGITS, 2, LP, N2, N1), DIGITS ** -0.5, 3.0, ((0, 4), (4, 2), (5, 2)))
    basis_up = scatter_about(keys[3], (DIGITS, LQ + LP, DLIMBS), DLIMBS ** -0.5, 3.5)
    basis_down = scatter_about(keys[4], (LQ, LP), LP ** -0.5, 3.0, ((0, 2),))
    special_inverse = jnp.clip(jnp.exp(math.log(2.0) - 1.3862944 * jax.random.uniform(keys[5], (LQ,), jnp.float32) ** shard_levels(keys[5], (LQ,), ((0, 2),), -0.2, 0.2)), 0.5, 2.0)
    parent_table = draw_parent_table(jax.random.fold_in(jax.random.fold_in(keys[8], part), 71), part)
    owner_table = draw_owner_table(jax.random.fold_in(jax.random.fold_in(keys[8], part), 71), part)
    return {"root_keys": root_keys, "switch_main": switch_main, "switch_special": switch_special, "basis_up": basis_up, "basis_down": basis_down, "special_inverse": special_inverse, "parent_table": parent_table, "owner_table": owner_table}


def cosine_table(length):
    frequency = jnp.arange(length).astype(jnp.float32)[:, None]
    sample = jnp.arange(length).astype(jnp.float32)[None, :]
    weight = jnp.where(frequency == 0, jnp.sqrt(1.0 / length), jnp.sqrt(2.0 / length))
    return (weight * jnp.cos(math.pi * (2.0 * sample + 1.0) * frequency / (2.0 * length))).astype(jnp.bfloat16)

def limb_twist(limb_ids):
    multiplier = 2 * limb_ids + 1
    product = multiplier[:, None, None] * jnp.arange(N1)[None, :, None] * jnp.arange(N2)[None, None, :] % N2
    return 1.0 + 0.5 * jnp.cos(2.0 * math.pi * product.astype(jnp.float32) / N2)

def forward(values, tables, twisting):
    short_cosine, long_cosine = tables
    halfway = jnp.einsum('...ab,kb->...ka', values.astype(jnp.float32), long_cosine.astype(jnp.float32))
    halfway = (halfway * jnp.swapaxes(twisting, -1, -2)).astype(jnp.bfloat16)
    return jnp.einsum('...kn,jn->...kj', halfway.astype(jnp.float32), short_cosine.astype(jnp.float32))

def inverse(values, tables, twisting):
    short_cosine, long_cosine = tables
    halfway = jnp.einsum('...kj,jn->...nk', values.astype(jnp.float32), short_cosine.astype(jnp.float32))
    halfway = (halfway / twisting).astype(jnp.bfloat16)
    return jnp.einsum('...nk,kb->...nb', halfway.astype(jnp.float32), long_cosine.astype(jnp.float32))

def derive(parent_key, main_key, special_key, basis_up, basis_down, special_inverse, tables, twist_all):
    twist_main = twist_all[:LQ]
    twist_special = twist_all[LQ:]
    digits = inverse(parent_key[:, 1], tables, twist_main).astype(jnp.bfloat16)
    digits = digits.reshape(COMPS, DIGITS, LQ // DIGITS, N1, N2)
    raised = jnp.einsum('cdsab,dts->cdtab', digits.astype(jnp.float32), basis_up.astype(jnp.float32)).astype(jnp.bfloat16)
    raised_hat = forward(raised, tables, twist_all)
    switch_all = jnp.concatenate([main_key, special_key], axis=2).astype(jnp.float32)
    summed = jnp.einsum('cdtkj,dqtkj->cqtkj', raised_hat, switch_all)
    upper_part = summed[:, :, LQ:].astype(jnp.bfloat16)
    lowered = inverse(upper_part, tables, twist_special).astype(jnp.bfloat16)
    converted = jnp.einsum('cqpab,lp->cqlab', lowered.astype(jnp.float32), basis_down.astype(jnp.float32)).astype(jnp.bfloat16)
    correction = forward(converted, tables, twist_main)
    result = (summed[:, :, :LQ] - correction) * special_inverse[None, None, :, None, None]
    leading = parent_key[:, 0].astype(jnp.float32) + result[:, 0]
    return jnp.stack([leading, result[:, 1]], axis=1).astype(jnp.bfloat16)

def reference(root_keys, switch_main, switch_special, basis_up, basis_down, special_inverse, parent_table, owner_table):
    tables = (cosine_table(N1), cosine_table(N2))
    twist_all = limb_twist(jnp.arange(LQ + LP))
    current = root_keys
    for tree_level in range(LEVELS):
        parents = jnp.take(current, parent_table[tree_level], axis=0)

        def derive_one(packed):
            return derive(packed[0], packed[1], packed[2], basis_up, basis_down, special_inverse, tables, twist_all)
        current = lax.map(derive_one, (parents, switch_main[:, tree_level], switch_special[:, tree_level]))
    position = jnp.arange(LEAVES)
    same_owner = owner_table[:, None] == owner_table[None, :]
    rank_within = lax.optimization_barrier(jnp.sum((same_owner & (position[:, None] < position[None, :])).astype(jnp.int32), axis=0))
    slot_ids = jnp.arange(LEAVES * CAP)
    matches = (owner_table[None, :] == (slot_ids // CAP)[:, None]) & (rank_within[None, :] == (slot_ids % CAP)[:, None])
    source = lax.optimization_barrier(jnp.sum(jnp.where(matches, position[None, :], 0), axis=1)).astype(jnp.int32)
    filled = jnp.any(matches, axis=1)
    gathered = jnp.take(current, source, axis=0)
    gathered = jnp.where(filled[:, None, None, None, None, None], gathered, jnp.zeros((), gathered.dtype))
    return gathered.reshape((LEAVES, CAP) + current.shape[1:])
```

```python
import functools
import math

import jax
import jax.numpy as jnp
from jax import lax
from jax.experimental import pallas as pl
from jax.experimental.pallas import tpu as pltpu
from jax.sharding import PartitionSpec as P

N1 = 128
N2 = 256
LQ = 12
LP = 4
DIGITS = 4
LEVELS = 2
RADIUS = 2
CAP = 3
DLIMBS = LQ // DIGITS


def cosine_table(length):
    frequency = jnp.arange(length).astype(jnp.float32)[:, None]
    sample = jnp.arange(length).astype(jnp.float32)[None, :]
    weight = jnp.where(frequency == 0, jnp.sqrt(1.0 / length), jnp.sqrt(2.0 / length))
    return (weight * jnp.cos(math.pi * (2.0 * sample + 1.0) * frequency / (2.0 * length))).astype(
        jnp.bfloat16
    )


def twist_table(first_col, cols):
    multiplier = 2 * jnp.arange(LQ + LP) + 1
    product = (
        multiplier[:, None, None]
        * (first_col + jnp.arange(cols))[None, :, None]
        * jnp.arange(N1)[None, None, :]
        % N2
    )
    return 1.0 + 0.5 * jnp.cos(2.0 * math.pi * product.astype(jnp.float32) / N2)


def dot(left, right):
    return jnp.dot(left, right, preferred_element_type=jnp.float32)


def accumulate(ids, up, raw, twist, table, table_t, keys, total, fresh):
    digit, base = ids[0], ids[1]
    halves = [
        dot(raw[s], table) / twist[base + s] for s in range(DLIMBS)
    ]
    slot = 0
    for group, key in enumerate(keys):
        for k in range(key.shape[2]):
            target = ids[2 + group] + k
            at = (digit * (LQ + LP) + target) * DLIMBS
            mixed = up[at] * halves[0]
            for s in range(1, DLIMBS):
                mixed = mixed + up[at + s] * halves[s]
            hat = dot((mixed * twist[target]).astype(jnp.bfloat16), table_t)
            for i in range(2):
                term = hat * key[0, i, k].astype(jnp.float32)
                total[i, slot] = term if fresh else total[i, slot] + term
            slot += 1


def digit_kernel(groups, fresh, ids, up, raw, twist, table, table_t, *rest):
    keys, total = rest[:groups], rest[-1]
    table, table_t = table[...], table_t[...]
    if not fresh:
        total[...] = rest[groups][...]
    accumulate(ids, up, raw, twist, table, table_t, keys, total, fresh)


def last_kernel(groups, pieces, ids, up, down, inverse, raw, twist, table, table_t, *rest):
    keys, before, first, outs, total = (
        rest[:groups],
        rest[groups],
        rest[groups + 1],
        rest[groups + 2 : -1],
        rest[-1],
    )
    table, table_t = table[...], table_t[...]
    total[...] = before[...]
    accumulate(ids, up, raw, twist, table, table_t, keys, total, False)
    lower = keys[0].shape[2]
    for i in (1, 0):
        residues = []
        slot = lower
        for group in range(1, groups):
            for k in range(keys[group].shape[2]):
                limb = ids[2 + group] + k
                part = dot(total[i, slot].astype(jnp.bfloat16), table) / twist[limb]
                residues.append((limb - LQ, part))
                slot += 1
        for q in range(lower):
            mixed = None
            for limb, part in residues:
                term = down[q * LP + limb] * part
                mixed = term if mixed is None else mixed + term
            mixed = (mixed * twist[ids[2] + q]).astype(jnp.bfloat16)
            value = (total[i, q] - dot(mixed, table_t)) * inverse[q]
            if i == 0:
                outs[0][q] = (first[q].astype(jnp.float32) + value).astype(jnp.bfloat16)
            else:
                outs[1 + q // pieces][q % pieces] = value.astype(jnp.bfloat16)


def smem():
    return pl.BlockSpec(memory_space=pltpu.SMEM)


def whole(shape):
    return pl.BlockSpec(shape, lambda g, ids: (0,) * len(shape))


def key_block(key):
    shape = (1,) + key.shape[1:]
    return pl.BlockSpec(shape, lambda g, ids: (ids[0],) + (0,) * (len(shape) - 1))


def cost(rows, arrays):
    size = sum(math.prod(a.shape) * a.dtype.itemsize for a in arrays)
    return pl.CostEstimate(flops=2 * rows * N1 * N1, bytes_accessed=size, transcendentals=0)


def add_digit(ids, up, raw, twist, tables, keys, total):
    targets = sum(k.shape[2] for k in keys)
    cols = raw.shape[1]
    fresh = total is None
    before = [] if fresh else [total]
    args = [raw, twist, tables[0], tables[1], *keys, *before]
    shape = (2, targets, cols, N1)
    specs = [smem(), whole(raw.shape), whole(twist.shape), whole((N1, N1)), whole((N1, N1))]
    specs += [key_block(k) for k in keys] + [whole(shape)] * len(before)
    return pl.pallas_call(
        functools.partial(digit_kernel, len(keys), fresh),
        grid_spec=pltpu.PrefetchScalarGridSpec(
            num_scalar_prefetch=1, grid=(1,), in_specs=specs, out_specs=whole(shape)
        ),
        out_shape=jax.ShapeDtypeStruct(shape, jnp.float32),
        cost_estimate=cost(targets * cols, args),
        compiler_params=pltpu.CompilerParams(vmem_limit_bytes=16 * 2**20),
        name="add_digit",
    )(ids, up, *args)


def finish(ids, up, down, inverse, raw, twist, tables, keys, total, first, pieces):
    lower, cols = first.shape[0], first.shape[1]
    args = [raw, twist, tables[0], tables[1], *keys, total, first]
    specs = [smem()] * 3
    specs += [whole(raw.shape), whole(twist.shape), whole((N1, N1)), whole((N1, N1))]
    specs += [key_block(k) for k in keys] + [whole(total.shape), whole(first.shape)]
    outs = [jax.ShapeDtypeStruct(first.shape, jnp.bfloat16)]
    outs += [jax.ShapeDtypeStruct((pieces, cols, N1), jnp.bfloat16)] * (lower // pieces)
    return pl.pallas_call(
        functools.partial(last_kernel, len(keys), pieces),
        grid_spec=pltpu.PrefetchScalarGridSpec(
            num_scalar_prefetch=1,
            grid=(1,),
            in_specs=specs,
            out_specs=[whole(o.shape) for o in outs],
            scratch_shapes=[pltpu.VMEM(total.shape, jnp.float32)],
        ),
        out_shape=outs,
        cost_estimate=cost(6 * lower * cols, args),
        compiler_params=pltpu.CompilerParams(vmem_limit_bytes=20 * 2**20),
        name="finish",
    )(ids, up, down, inverse, *args)


def shifted(value, axis, offset):
    size = lax.axis_size(axis)
    return lax.ppermute(value, axis, [((i + offset) % size, i) for i in range(size)])


def paired(value, axis):
    size = lax.axis_size(axis)
    return lax.ppermute(value, axis, [(i ^ 1, i) for i in range(size)])


def fetch(chunks, parents):
    leaves = lax.axis_size("leaf")
    me = lax.axis_index("leaf")
    parent = parents[me]
    if leaves != 2 * RADIUS:
        offsets = [e for e in range(-RADIUS, RADIUS + 1) if e != 0]
        found = []
        for chunk in chunks:
            value = chunk
            for e in offsets:
                value = jnp.where(parent == (me + e) % leaves, shifted(chunk, "leaf", e), value)
            found.append(value)
        return found
    served = parents[(me + RADIUS) % leaves]
    beside = [paired(chunk, "leaf") for chunk in chunks]
    across = [
        shifted(jnp.where(served == me ^ 1, b, c), "leaf", RADIUS) for b, c in zip(beside, chunks)
    ]
    return [
        jnp.where(parent == me, c, jnp.where(parent == me ^ 1, b, a))
        for a, b, c in zip(across, beside, chunks)
    ]


def deliver(key, source, filled):
    leaves = lax.axis_size("leaf")
    me = lax.axis_index("leaf")
    if leaves != 2 * RADIUS:
        flat = key.reshape(leaves, -1, N1)
        spread = lax.all_to_all(flat, "leaf", split_axis=0, concat_axis=0, tiled=True)
        chosen = jnp.take(spread, source, axis=0)
        chosen = jnp.where(filled[:, None, None], chosen, jnp.zeros((), chosen.dtype))
        chosen = chosen.reshape(leaves, CAP, spread.shape[1], N1)
        back = lax.all_to_all(chosen, "leaf", split_axis=0, concat_axis=0, tiled=True)
        return jnp.swapaxes(back, 0, 1).reshape((CAP,) + key.shape)
    across = shifted(key, "leaf", RADIUS)
    beside = paired(key, "leaf")
    corner = paired(across, "leaf")
    own_source = lax.dynamic_slice_in_dim(source, me * CAP, CAP)
    own_filled = lax.dynamic_slice_in_dim(filled, me * CAP, CAP)
    slots = []
    for s in range(CAP):
        value = jnp.where(own_source[s] == (me ^ 1) ^ RADIUS, corner, key)
        value = jnp.where(own_source[s] == me ^ RADIUS, across, value)
        value = jnp.where(own_source[s] == me ^ 1, beside, value)
        slots.append(jnp.where(own_filled[s], value, jnp.zeros((), key.dtype)))
    return jnp.stack(slots)


def per_device(
    root_keys,
    switch_main,
    switch_special,
    basis_up,
    basis_down,
    special_inverse,
    parent_table,
    owner_table,
):
    leaves = lax.axis_size("leaf")
    limbs = lax.axis_size("limb")
    me = lax.axis_index("limb")
    lower, cols = root_keys.shape[3], root_keys.shape[4]
    upper = switch_special.shape[4]
    held = lower // DLIMBS
    short = cosine_table(N1)
    tables = (short, short.T)
    twist = twist_table(lax.axis_index("coef") * cols, cols)
    up = basis_up.astype(jnp.float32).reshape(-1)
    down = basis_down.astype(jnp.float32).reshape(-1)
    first = root_keys[0, 0, 0]
    chunks = [root_keys[0, 0, 1, h * DLIMBS : (h + 1) * DLIMBS] for h in range(held)]
    holders = [(me + r) % limbs for r in range(limbs)]
    firsts = [me * lower] + [LQ + holder * upper for holder in holders]
    for level in range(LEVELS):
        special = switch_special[0, level]
        keys = [switch_main[0, level], special]
        keys += [shifted(special, "limb", r) for r in range(1, limbs)]
        parents = parent_table[level]
        mine = fetch(chunks, parents)
        (parent_first,) = fetch([first], parents)
        steps = [(0, h, mine[h]) for h in range(held)]
        for r in range(1, limbs):
            steps += [(r, h, shifted(mine[h], "limb", r)) for h in range(held)]
        total = None
        for r, h, raw in steps:
            digit = holders[r] * held + h
            ids = jnp.stack([digit, digit * DLIMBS] + firsts).astype(jnp.int32)
            if (r, h) != (limbs - 1, held - 1):
                total = add_digit(ids, up, raw, twist, tables, keys, total)
            else:
                pieces = lower if level == LEVELS - 1 else DLIMBS
                first, *chunks = finish(
                    ids, up, down, special_inverse, raw, twist, tables, keys, total,
                    parent_first, pieces,
                )
    current = jnp.stack([first, chunks[0]])
    position = jnp.arange(leaves)
    same_owner = owner_table[:, None] == owner_table[None, :]
    rank_within = jnp.sum(
        (same_owner & (position[:, None] < position[None, :])).astype(jnp.int32), axis=0
    )
    slot_ids = jnp.arange(leaves * CAP)
    matches = (owner_table[None, :] == (slot_ids // CAP)[:, None]) & (
        rank_within[None, :] == (slot_ids % CAP)[:, None]
    )
    source = jnp.sum(jnp.where(matches, position[None, :], 0), axis=1)
    filled = jnp.any(matches, axis=1)
    delivered = deliver(current, source, filled)
    return delivered[None, :, None]


def solution(mesh):
    return jax.shard_map(
        per_device,
        mesh=mesh,
        in_specs=(
            P(("grp", "leaf"), None, None, "limb", "coef", None),
            P(("grp", "leaf"), None, None, None, "limb", "coef", None),
            P(("grp", "leaf"), None, None, None, "limb", "coef", None),
            P(),
            P("limb", None),
            P("limb"),
            P(None, "grp"),
            P("grp"),
        ),
        out_specs=P(("grp", "leaf"), None, None, None, "limb", "coef", None),
        check_vma=False,
    )
```
